512 devices in a mesh: wide: 32 (over y, x_hi, core), pair: 16 (over x_lo, z).
Axes of the slice: x: 4 (x_hi: 2, x_lo: 2; x = x_hi * 2 + x_lo), y: 8, z: 8, core: 2. Of those that a mesh axis runs over, the one named last changes fastest.
Arguments:
- rhs: bfloat16 [524288, 512], P(('wide', 'pair')), may hold values from -6 to 6
- coords: bfloat16 [1024, 2, 512], P(('wide', 'pair')), may hold values from 0 to 1
- near_index: int32 [1024, 3], P(('wide', 'pair')), may hold values from -2 to 2, as said below
- project_basis: bfloat16 [1024, 512, 192], P(('wide', 'pair')), may hold values from -0.25 to 0.25
- expand_basis: bfloat16 [1024, 512, 192], P(('wide', 'pair')), may hold values from -0.4375 to 0.4375
- transfer: bfloat16 [512, 5, 2, 192, 192], P(('wide', 'pair')), may hold values from -0.3125 to 0.3125
- level_perm: int32 [5, 192], replicated, may hold values from 0 to 191, each once within a row
Outputs:
- applied: bfloat16 [524288, 512], P(('wide', 'pair'))
The draws below stay inside these ranges and needn't reach their ends.
Inputs may be any that keep to these rules, and one draw needn't show every extreme that they name: `near_index`: each row holds 3 different offsets. `level_perm`: each row is a permutation of 0 to 191.
All inputs are finite; a program needn't handle non-finite values.
Results may differ from the reference program's by a relative error of at most 0.0095.
Values may be sent and summed in bfloat16 or wider, within the bound.
No kernel may reach another device: no remote copies, remote signals or barrier semaphores. Data moves between devices by JAX's collectives and lax.ppermute only.
A program may use at most 64 MiB of HBM per device.

```python
import math
import jax
import jax.numpy as jnp
from jax import lax

LEAF = 512
LEAVES_DEV = 2
RANK = 192
COLS = 512
NB = 3
LW = 3
LP = 2
DEVICES_ALL = 512
NLEAVES = 1024
UNKNOWNS = 524288
N_WIDE = 32
N_PAIR = 16


def draw_near_index(key, part):
    scores = jax.random.randint(key, (NLEAVES, 5), 0, 4096) * 5 + jnp.arange(5, dtype=jnp.int32)[None, :]
    chosen = lax.top_k(scores, NB)[1]
    return (chosen - 2).astype(jnp.int32)


def level_of(rng, dims, shards, least, top_value):
    gain = 1.0
    for position, blocks in shards:
        draws = jax.random.uniform(jax.random.fold_in(jax.random.fold_in(rng, 6), position), (blocks,), jnp.float32, least / len(shards), top_value / len(shards))
        gain = gain * jnp.repeat(jnp.exp(draws), dims[position] // blocks).reshape((-1,) + (1,) * (len(dims) - 1 - position))
    return gain


def bell_draw(stream_key, shape, width, bound, cuts=(), held_as=jnp.bfloat16):
    entries = jax.random.normal(stream_key, shape, jnp.float32) * width
    if len(cuts) > 0:
        entries = level_of(stream_key, shape, cuts, -0.22, 0.18) * entries
    return jnp.clip(entries, min=-bound, max=bound).astype(held_as)


def setup_inputs(seed: int = 0) -> dict:
    key_list = jax.random.split(jax.random.key(seed), 8)
    rhs = bell_draw(key_list[0], (UNKNOWNS, COLS), 1.0, 6.0, ((0, 512),))
    coords = jnp.clip(1.0 * jax.random.uniform(key_list[1], (NLEAVES, 2, LEAF), jnp.float32) ** level_of(key_list[1], (NLEAVES, 2, LEAF), ((0, 512),), -0.2, 0.2), 0.0, 1.0).astype(jnp.bfloat16)
    near_index = draw_near_index(jax.random.fold_in(key_list[7], 71), 0)
    project_basis = bell_draw(key_list[3], (NLEAVES, LEAF, RANK), LEAF ** -0.5, 0.25, ((0, 512),))
    expand_basis = bell_draw(key_list[4], (NLEAVES, LEAF, RANK), RANK ** -0.5, 0.4375, ((0, 512),))
    transfer = bell_draw(key_list[5], (DEVICES_ALL, LW + LP, 2, RANK, RANK), (2 * RANK) ** -0.5, 0.3125, ((0, 512),))
    level_perm = jax.vmap(lambda own: jax.random.permutation(own, RANK))(jax.random.split(key_list[6], (LW + LP))).reshape((LW + LP, RANK)).astype(jnp.int32)
    return dict(rhs=rhs, coords=coords, near_index=near_index, project_basis=project_basis, expand_basis=expand_basis, transfer=transfer, level_perm=level_perm)


softening = 0.0004

def kernel_tile(target, source):
    delta_x = target[0][:, None] - source[0][None, :]
    delta_y = target[1][:, None] - source[1][None, :]
    factor = 0.25 / math.sqrt(target.shape[1])
    return (lax.rsqrt(delta_x * delta_x + delta_y * delta_y + softening) * factor).astype(jnp.bfloat16)

def reference(rhs, coords, near_index, project_basis, expand_basis, transfer, level_perm):
    nleaves = coords.shape[0]
    columns = rhs.shape[1]
    leaves = rhs.reshape(nleaves, LEAF, columns)
    points = coords.astype(jnp.float32)

    def near_leaf(target):
        summed = jnp.zeros((LEAF, columns), jnp.float32)
        for slot in range(NB):
            source = target + near_index[target, slot]
            inside = (source >= 0) & (source < nleaves)
            clipped = jnp.clip(source, 0, nleaves - 1).astype(jnp.int32)
            tile = kernel_tile(points[target], points[clipped])
            product = jnp.dot(tile, leaves[clipped], preferred_element_type=jnp.float32)
            summed = summed + jnp.where(inside, product, jnp.zeros_like(product))
        return summed
    nearby = lax.map(near_leaf, jnp.arange(nleaves, dtype=jnp.int32))
    devices = N_WIDE * N_PAIR
    projected = jnp.einsum('nlr,nlc->nrc', project_basis.astype(jnp.float32), leaves.astype(jnp.float32))
    projected = projected.reshape(devices, LEAVES_DEV, RANK, columns)
    projected = (projected[:, 0] + projected[:, 1]).astype(jnp.bfloat16)
    device_ids = jnp.arange(devices, dtype=jnp.int32)
    wide_id = device_ids // N_PAIR
    pair_id = device_ids % N_PAIR
    for level in range(LW + LP):
        if level < LW:
            partner = jnp.bitwise_xor(wide_id, 1 << level) * N_PAIR + pair_id
        else:
            partner = wide_id * N_PAIR + jnp.bitwise_xor(pair_id, 1 << level - LW)
        partner_rows = projected[partner][:, level_perm[level], :]
        updated = jnp.einsum('drs,dsc->drc', transfer[:, level, 0].astype(jnp.float32), projected.astype(jnp.float32))
        updated = updated + jnp.einsum('drs,dsc->drc', transfer[:, level, 1].astype(jnp.float32), partner_rows.astype(jnp.float32))
        projected = updated.astype(jnp.bfloat16)
    expand_rows = expand_basis.reshape(devices, LEAVES_DEV * LEAF, RANK).astype(jnp.float32)
    distant = jnp.einsum('dlr,drc->dlc', expand_rows, projected.astype(jnp.float32))
    summed = nearby.reshape(-1, columns) + distant.reshape(-1, columns)
    return summed.astype(jnp.bfloat16)
```

```python
import math

import jax
import jax.numpy as jnp
from jax import lax
from jax.experimental import pallas as pl
from jax.experimental.pallas import tpu as pltpu
from jax.sharding import PartitionSpec as P

LW = 3
LP = 2
LEVELS = LW + LP
LEAF = 512
RANK = 192
COLS = 512
ROWS = 1024
PACK = ROWS + 16
SOFT = 0.0004
FACTOR = 0.25 / math.sqrt(LEAF)
F32 = jnp.float32
BF16 = jnp.bfloat16
VMEM = pl.BlockSpec(memory_space=pltpu.VMEM)
SMEM = pl.BlockSpec(memory_space=pltpu.SMEM)


def params():
    return pltpu.CompilerParams(vmem_limit_bytes=40 << 20)


def project_kernel(x_ref, basis_ref, coords_ref, s_ref, pack_ref):
    total = jnp.dot(basis_ref[0], x_ref[:LEAF, :], preferred_element_type=F32)
    total = total + jnp.dot(basis_ref[1], x_ref[LEAF:, :], preferred_element_type=F32)
    s_ref[...] = total.astype(BF16)
    pack_ref[:ROWS, :] = x_ref[...]
    pack_ref[ROWS:, :] = jnp.concatenate(
        [coords_ref[...], jnp.zeros((12, COLS), BF16)], axis=0
    )


def project(x, basis_t, coords4):
    return pl.pallas_call(
        project_kernel,
        out_shape=(
            jax.ShapeDtypeStruct((RANK, COLS), BF16),
            jax.ShapeDtypeStruct((PACK, COLS), BF16),
        ),
        in_specs=[VMEM, VMEM, VMEM],
        out_specs=(VMEM, VMEM),
        compiler_params=params(),
        name="project",
    )(x, basis_t, coords4)


def prepare_kernel(transfer_ref, perm_ref, expand_ref, t_ref, e_ref):
    k = lax.broadcasted_iota(jnp.int32, (RANK, RANK), 0)
    for level in range(LEVELS):
        t_ref[level, 0] = transfer_ref[level, 0]
        picked = jnp.where(k == perm_ref[level : level + 1, :], 1.0, 0.0).astype(BF16)
        t_ref[level, 1] = lax.dot_general(
            transfer_ref[level, 1], picked, (((1,), (1,)), ((), ())), preferred_element_type=F32
        ).astype(BF16)
    for leaf in range(2):
        e_ref[leaf * LEAF : (leaf + 1) * LEAF, :] = expand_ref[leaf].T


def prepare(transfer, perm, expand_t):
    return pl.pallas_call(
        prepare_kernel,
        out_shape=(
            jax.ShapeDtypeStruct((LEVELS, 2, RANK, RANK), BF16),
            jax.ShapeDtypeStruct((ROWS, RANK), BF16),
        ),
        in_specs=[VMEM, VMEM, VMEM],
        out_specs=(VMEM, VMEM),
        compiler_params=params(),
        name="prepare",
    )(transfer, perm, expand_t)


def level_kernel(t_ref, own_ref, other_ref, s_ref):
    total = jnp.dot(t_ref[0, 0], own_ref[...], preferred_element_type=F32)
    total = total + jnp.dot(t_ref[0, 1], other_ref[...], preferred_element_type=F32)
    s_ref[...] = total.astype(BF16)


def level_step(level, t, own, other):
    return pl.pallas_call(
        level_kernel,
        grid=(1,),
        out_shape=jax.ShapeDtypeStruct((RANK, COLS), BF16),
        in_specs=[
            pl.BlockSpec((1, 2, RANK, RANK), lambda i: (level, 0, 0, 0)),
            pl.BlockSpec((RANK, COLS), lambda i: (0, 0)),
            pl.BlockSpec((RANK, COLS), lambda i: (0, 0)),
        ],
        out_specs=pl.BlockSpec((RANK, COLS), lambda i: (0, 0)),
        compiler_params=params(),
        name=f"level{level}",
    )(t, own, other)


def near_kernel(index_ref, own_ref, low_ref, high_ref, near_ref):
    sides = (low_ref, own_ref, high_ref)
    scale = 1.0 / FACTOR
    points = own_ref[ROWS : ROWS + 8, :].astype(F32) * scale
    columns = points.T
    rows = [side[ROWS : ROWS + 8, :].astype(F32) * scale for side in sides]
    for target in range(2):
        block = pl.ds(target * LEAF, LEAF)
        near_ref[block, :] = jnp.zeros((LEAF, COLS), F32)
        tx = columns[:, 2 * target : 2 * target + 1]
        ty = columns[:, 2 * target + 1 : 2 * target + 2]
        for offset in (0, 1, -1, 2, -2):
            side, leaf = divmod(target + offset + 2, 2)
            used = (
                (index_ref[target, 0] == offset)
                | (index_ref[target, 1] == offset)
                | (index_ref[target, 2] == offset)
            )

            @pl.when(used)
            def _(side=side, leaf=leaf, tx=tx, ty=ty, block=block):
                sx = rows[side][2 * leaf : 2 * leaf + 1, :]
                sy = rows[side][2 * leaf + 1 : 2 * leaf + 2, :]
                dx = tx - sx
                dy = ty - sy
                tile = lax.rsqrt(dx * dx + dy * dy + SOFT * scale * scale).astype(BF16)
                near_ref[block, :] += jnp.dot(
                    tile,
                    sides[side][leaf * LEAF : (leaf + 1) * LEAF, :],
                    preferred_element_type=F32,
                )


def near_field(index, own, low, high):
    return pl.pallas_call(
        near_kernel,
        out_shape=jax.ShapeDtypeStruct((ROWS, COLS), F32),
        in_specs=[SMEM, VMEM, VMEM, VMEM],
        out_specs=VMEM,
        compiler_params=params(),
        name="near",
    )(index, own, low, high)


def final_kernel(t_ref, own_ref, other_ref, e_ref, near_ref, out_ref, s_ref):
    @pl.when(pl.program_id(0) == 0)
    def _():
        total = jnp.dot(t_ref[0, 0], own_ref[...], preferred_element_type=F32)
        total = total + jnp.dot(t_ref[0, 1], other_ref[...], preferred_element_type=F32)
        s_ref[...] = total.astype(BF16)

    distant = jnp.dot(e_ref[...], s_ref[...], preferred_element_type=F32)
    out_ref[...] = (near_ref[...] + distant).astype(BF16)


def final_step(t, own, other, e, near):
    block = 256
    return pl.pallas_call(
        final_kernel,
        grid=(ROWS // block,),
        out_shape=jax.ShapeDtypeStruct((ROWS, COLS), BF16),
        in_specs=[
            pl.BlockSpec((1, 2, RANK, RANK), lambda i: (LEVELS - 1, 0, 0, 0)),
            pl.BlockSpec((RANK, COLS), lambda i: (0, 0)),
            pl.BlockSpec((RANK, COLS), lambda i: (0, 0)),
            pl.BlockSpec((block, RANK), lambda i: (i, 0)),
            pl.BlockSpec((block, COLS), lambda i: (i, 0)),
        ],
        out_specs=pl.BlockSpec((block, COLS), lambda i: (i, 0)),
        scratch_shapes=[pltpu.VMEM((RANK, COLS), BF16)],
        compiler_params=params(),
        name="final",
    )(t, own, other, e, near)


def from_partner(block, axis, bit):
    count = lax.axis_size(axis)
    return lax.ppermute(block, axis, [(i, i ^ (1 << bit)) for i in range(count)])


def on_device(rhs, coords, near_index, project_basis, expand_basis, transfer, level_perm):
    axes = ("wide", "pair")
    devices = lax.axis_size("wide") * lax.axis_size("pair")
    up = [(i, i + 1) for i in range(devices - 1)]
    down = [(i + 1, i) for i in range(devices - 1)]
    s, pack = project(rhs, jnp.swapaxes(project_basis, 1, 2), coords.reshape(4, LEAF))
    partner = from_partner(s, "wide", 0)
    low = lax.ppermute(pack, axes, up)
    high = lax.ppermute(pack, axes, down)
    t, e = prepare(transfer[0], level_perm, jnp.swapaxes(expand_basis, 1, 2))
    for level in range(LEVELS - 1):
        s = level_step(level, t, s, partner)
        if level + 1 < LW:
            partner = from_partner(s, "wide", level + 1)
        else:
            partner = from_partner(s, "pair", level + 1 - LW)
    near = near_field(near_index, pack, low, high)
    return final_step(t, s, partner, e, near)


def solution(mesh):
    return jax.shard_map(
        on_device,
        mesh=mesh,
        in_specs=(
            P(("wide", "pair"), None),
            P(("wide", "pair"), None, None),
            P(("wide", "pair"), None),
            P(("wide", "pair"), None, None),
            P(("wide", "pair"), None, None),
            P(("wide", "pair"), None, None, None, None),
            P(),
        ),
        out_specs=P(("wide", "pair"), None),
        check_vma=False,
    )
```

```python
import math

import jax
import jax.numpy as jnp
from jax import lax
from jax.experimental import pallas as pl
from jax.experimental.pallas import tpu as pltpu
from jax.sharding import PartitionSpec as P

LW = 3
LP = 2
LEVELS = LW + LP
LEAF = 512
RANK = 192
COLS = 512
ROWS = 1024
PACK = ROWS + 16
COVER = 30_000_000_000
SOFT = 0.0004
FACTOR = 0.25 / math.sqrt(LEAF)
F32 = jnp.float32
BF16 = jnp.bfloat16
VMEM = pl.BlockSpec(memory_space=pltpu.VMEM)
HBM = pl.BlockSpec(memory_space=pltpu.HBM)
SMEM = pl.BlockSpec(memory_space=pltpu.SMEM)


def in_hbm(array):
    return pltpu.with_memory_space_constraint(array, pltpu.HBM)


def params():
    return pltpu.CompilerParams(vmem_limit_bytes=40 << 20)


def folded(matrix, perm_row):
    k = lax.broadcasted_iota(jnp.int32, (RANK, RANK), 0)
    picked = jnp.where(k == perm_row, 1.0, 0.0).astype(BF16)
    return lax.dot_general(
        matrix, picked, (((1,), (1,)), ((), ())), preferred_element_type=F32
    ).astype(BF16)


def project_kernel(
    x_ref,
    basis_ref,
    points_ref,
    transfer_ref,
    order_ref,
    s_ref,
    pack_ref,
    t_ref,
    b_ref,
    coords_ref,
    perm_ref,
    sems,
):
    copies = []
    for leaf in range(2):
        block = pl.ds(leaf * LEAF, LEAF)
        copies.append(
            (
                pltpu.make_async_copy(basis_ref.at[leaf], b_ref.at[leaf], sems.at[2 * leaf]),
                pltpu.make_async_copy(
                    x_ref.at[block], pack_ref.at[block], sems.at[2 * leaf + 1]
                ),
            )
        )
    points = pltpu.make_async_copy(points_ref, coords_ref, sems.at[4])
    first = pltpu.make_async_copy(transfer_ref.at[0], t_ref.at[0], sems.at[5])
    order = pltpu.make_async_copy(order_ref, perm_ref, sems.at[6])
    for pair in copies:
        for copy in pair:
            copy.start()
    points.start()
    first.start()
    order.start()
    points.wait()
    pack_ref[ROWS:, :] = jnp.concatenate(
        [coords_ref[0], coords_ref[1], jnp.zeros((12, COLS), BF16)], axis=0
    )
    total = None
    for leaf in range(2):
        for copy in copies[leaf]:
            copy.wait()
        part = jnp.dot(
            b_ref[leaf], pack_ref[leaf * LEAF : (leaf + 1) * LEAF, :], preferred_element_type=F32
        )
        total = part if total is None else total + part
    s_ref[...] = total.astype(BF16)
    first.wait()
    order.wait()
    t_ref[0, 1] = folded(t_ref[0, 1], perm_ref[0:1, :])


def project(x, basis_t, coords, transfer, perm):
    return pl.pallas_call(
        project_kernel,
        out_shape=(
            jax.ShapeDtypeStruct((RANK, COLS), BF16),
            jax.ShapeDtypeStruct((PACK, COLS), BF16),
            jax.ShapeDtypeStruct((1, 2, RANK, RANK), BF16),
        ),
        in_specs=[HBM] * 5,
        out_specs=(VMEM, VMEM, VMEM),
        scratch_shapes=[
            pltpu.VMEM((2, RANK, LEAF), BF16),
            pltpu.VMEM((2, 2, LEAF), BF16),
            pltpu.VMEM((LEVELS, RANK), jnp.int32),
            pltpu.SemaphoreType.DMA((7,)),
        ],
        compiler_params=params(),
        name="project",
    )(*(in_hbm(array) for array in (x, basis_t, coords, transfer, perm)))


def prepare_kernel(transfer_ref, perm_ref, expand_ref, after_ref, t_ref, e_ref):
    for level in range(1, LEVELS):
        t_ref[level - 1, 0] = transfer_ref[level, 0]
        t_ref[level - 1, 1] = folded(transfer_ref[level, 1], perm_ref[level : level + 1, :])
    for leaf in range(2):
        e_ref[leaf * LEAF : (leaf + 1) * LEAF, :] = expand_ref[leaf].T


def prepare(transfer, perm, expand_t, after):
    return pl.pallas_call(
        prepare_kernel,
        out_shape=(
            jax.ShapeDtypeStruct((LEVELS - 1, 2, RANK, RANK), BF16),
            jax.ShapeDtypeStruct((ROWS, RANK), BF16),
        ),
        in_specs=[VMEM, VMEM, VMEM, VMEM],
        out_specs=(VMEM, VMEM),
        compiler_params=params(),
        name="prepare",
    )(transfer, perm, expand_t, after)


def level_kernel(t_ref, own_ref, other_ref, s_ref):
    total = jnp.dot(t_ref[0, 0], own_ref[...], preferred_element_type=F32)
    total = total + jnp.dot(t_ref[0, 1], other_ref[...], preferred_element_type=F32)
    s_ref[...] = total.astype(BF16)


def gathered_kernel(high_ref, t_ref, own_ref, both_ref, s_ref):
    total = jnp.dot(t_ref[0, 0], own_ref[...], preferred_element_type=F32)
    total = total + jnp.dot(
        t_ref[0, 1], both_ref[1 - high_ref[0]], preferred_element_type=F32
    )
    s_ref[...] = total.astype(BF16)


def level_step(t, index, own, other, high=None, weight=4 * RANK * RANK * COLS):
    flat = pl.BlockSpec((RANK, COLS), lambda i: (0, 0))
    specs = [pl.BlockSpec((1, 2, RANK, RANK), lambda i: (index, 0, 0, 0)), flat]
    if high is None:
        body, specs, args = level_kernel, specs + [flat], (t, own, other)
    else:
        both = pl.BlockSpec((2, RANK, COLS), lambda i: (0, 0, 0))
        body, specs, args = gathered_kernel, [SMEM] + specs + [both], (high, t, own, other)
    return pl.pallas_call(
        body,
        grid=(1,),
        out_shape=jax.ShapeDtypeStruct((RANK, COLS), BF16),
        in_specs=specs,
        out_specs=flat,
        compiler_params=params(),
        cost_estimate=pl.CostEstimate(
            flops=weight, transcendentals=0, bytes_accessed=6 * RANK * COLS
        ),
        name=f"level_{index}",
    )(*args)


def near_kernel(index_ref, own_ref, low_ref, high_ref, near_ref):
    sides = (low_ref, own_ref, high_ref)
    scale = 1.0 / FACTOR
    points = own_ref[ROWS : ROWS + 8, :].astype(F32) * scale
    columns = points.T
    rows = [side[ROWS : ROWS + 8, :].astype(F32) * scale for side in sides]
    for target in range(2):
        block = pl.ds(target * LEAF, LEAF)
        near_ref[block, :] = jnp.zeros((LEAF, COLS), F32)
        tx = columns[:, 2 * target : 2 * target + 1]
        ty = columns[:, 2 * target + 1 : 2 * target + 2]
        for offset in (0, 1, -1, 2, -2):
            side, leaf = divmod(target + offset + 2, 2)
            used = (
                (index_ref[target, 0] == offset)
                | (index_ref[target, 1] == offset)
                | (index_ref[target, 2] == offset)
            )

            @pl.when(used)
            def _(side=side, leaf=leaf, tx=tx, ty=ty, block=block):
                sx = rows[side][2 * leaf : 2 * leaf + 1, :]
                sy = rows[side][2 * leaf + 1 : 2 * leaf + 2, :]
                dx = tx - sx
                dy = ty - sy
                tile = lax.rsqrt(dx * dx + dy * dy + SOFT * scale * scale).astype(BF16)
                near_ref[block, :] += jnp.dot(
                    tile,
                    sides[side][leaf * LEAF : (leaf + 1) * LEAF, :],
                    preferred_element_type=F32,
                )


def near_field(index, own, low, high):
    return pl.pallas_call(
        near_kernel,
        out_shape=jax.ShapeDtypeStruct((ROWS, COLS), F32),
        in_specs=[SMEM, VMEM, VMEM, VMEM],
        out_specs=VMEM,
        compiler_params=params(),
        name="near",
    )(index, own, low, high)


def final_kernel(t_ref, own_ref, other_ref, e_ref, near_ref, out_ref, s_ref):
    @pl.when(pl.program_id(0) == 0)
    def _():
        total = jnp.dot(t_ref[0, 0], own_ref[...], preferred_element_type=F32)
        total = total + jnp.dot(t_ref[0, 1], other_ref[...], preferred_element_type=F32)
        s_ref[...] = total.astype(BF16)

    distant = jnp.dot(e_ref[...], s_ref[...], preferred_element_type=F32)
    out_ref[...] = (near_ref[...] + distant).astype(BF16)


def final_step(t, own, other, e, near):
    block = 256
    return pl.pallas_call(
        final_kernel,
        grid=(ROWS // block,),
        out_shape=jax.ShapeDtypeStruct((ROWS, COLS), BF16),
        in_specs=[
            pl.BlockSpec((1, 2, RANK, RANK), lambda i: (LEVELS - 2, 0, 0, 0)),
            pl.BlockSpec((RANK, COLS), lambda i: (0, 0)),
            pl.BlockSpec((RANK, COLS), lambda i: (0, 0)),
            pl.BlockSpec((block, RANK), lambda i: (i, 0)),
            pl.BlockSpec((block, COLS), lambda i: (i, 0)),
        ],
        out_specs=pl.BlockSpec((block, COLS), lambda i: (i, 0)),
        scratch_shapes=[pltpu.VMEM((RANK, COLS), BF16)],
        compiler_params=params(),
        name="final",
    )(t, own, other, e, near)


def from_partner(block, axis, bit):
    count = lax.axis_size(axis)
    return lax.ppermute(block, axis, [(i, i ^ (1 << bit)) for i in range(count)])


def with_partner(block, axis, bit):
    count = lax.axis_size(axis)
    pairs = [[i, i | 1 << bit] for i in range(count) if not i >> bit & 1]
    both = lax.all_gather(block, axis, axis_index_groups=pairs)
    high = (lax.axis_index(axis) >> bit & 1).reshape(1)
    return both, high


def on_device(rhs, coords, near_index, project_basis, expand_basis, transfer, level_perm):
    axes = ("wide", "pair")
    devices = lax.axis_size("wide") * lax.axis_size("pair")
    up = [(i, i + 1) for i in range(devices - 1)]
    down = [(i + 1, i) for i in range(devices - 1)]
    s, pack, t0 = project(
        rhs, jnp.swapaxes(project_basis, 1, 2), coords, transfer[0], level_perm
    )
    both, high_bit = with_partner(s, "wide", 0)
    s = level_step(t0, 0, s, both, high_bit)
    partner = from_partner(s, "wide", 1)
    t, e = prepare(transfer[0], level_perm, jnp.swapaxes(expand_basis, 1, 2), s)
    sent, e = lax.optimization_barrier((pack, e))
    low = lax.ppermute(sent, axes, up)
    high = lax.ppermute(sent, axes, down)
    s = level_step(t, 0, s, partner, weight=COVER)
    s = level_step(t, 1, s, from_partner(s, "wide", 2))
    both, high_bit = with_partner(s, "pair", 0)
    s = level_step(t, 2, s, both, high_bit)
    partner = from_partner(s, "pair", 1)
    near = near_field(near_index, pack, low, high)
    return final_step(t, s, partner, e, near)


def solution(mesh):
    return jax.shard_map(
        on_device,
        mesh=mesh,
        in_specs=(
            P(("wide", "pair"), None),
            P(("wide", "pair"), None, None),
            P(("wide", "pair"), None),
            P(("wide", "pair"), None, None),
            P(("wide", "pair"), None, None),
            P(("wide", "pair"), None, None, None, None),
            P(),
        ),
        out_specs=P(("wide", "pair"), None),
        check_vma=False,
    )
```

```python
import functools
import math

import jax
import jax.numpy as jnp
from jax import lax
from jax.experimental import pallas as pl
from jax.experimental.pallas import tpu as pltpu
from jax.sharding import PartitionSpec as P

LW = 3
LP = 2
LEVELS = LW + LP
LEAF = 512
RANK = 192
COLS = 512
ROWS = 1024
PACK = ROWS + 16
RUN = 8
COVER_1 = 3_000_000_000
COVER_INNER = 5_000_000_000
COVER_OUTER = 6_000_000_000
COVER_FAR = 4_000_000_000
SOFT = 0.0004
FACTOR = 0.25 / math.sqrt(LEAF)
F32 = jnp.float32
BF16 = jnp.bfloat16
VMEM = pl.BlockSpec(memory_space=pltpu.VMEM)
HBM = pl.BlockSpec(memory_space=pltpu.HBM)
ANY = pl.BlockSpec(memory_space=pl.ANY)
SMEM = pl.BlockSpec(memory_space=pltpu.SMEM)


def in_hbm(array):
    return pltpu.with_memory_space_constraint(array, pltpu.HBM)


def in_vmem(array):
    return pltpu.with_memory_space_constraint(array, pltpu.VMEM)


def params():
    return pltpu.CompilerParams(vmem_limit_bytes=16 << 20)


def folded(matrix, perm_row):
    k = lax.broadcasted_iota(jnp.int32, (RANK, RANK), 0)
    picked = jnp.where(k == perm_row, 1.0, 0.0).astype(BF16)
    return lax.dot_general(
        matrix, picked, (((1,), (1,)), ((), ())), preferred_element_type=F32
    ).astype(BF16)


def project_kernel(
    x_ref,
    basis_ref,
    points_ref,
    transfer_ref,
    order_ref,
    s_ref,
    pack_ref,
    rows_ref,
    t_ref,
    basis_buf,
    coords_ref,
    perm_ref,
    sems,
):
    points = pltpu.make_async_copy(points_ref, coords_ref, sems.at[0])
    first = pltpu.make_async_copy(transfer_ref.at[0], t_ref.at[0], sems.at[1])
    order = pltpu.make_async_copy(order_ref, perm_ref, sems.at[2])
    copies = []
    for leaf in range(2):
        block = pl.ds(leaf * LEAF, LEAF)
        copies.append(
            (
                pltpu.make_async_copy(basis_ref.at[leaf], basis_buf.at[leaf], sems.at[3 + leaf]),
                pltpu.make_async_copy(x_ref.at[block], pack_ref.at[block], sems.at[5 + leaf]),
            )
        )
    points.start()
    for pair in copies:
        for copy in pair:
            copy.start()
    first.start()
    order.start()
    points.wait()
    rows_ref[...] = jnp.concatenate(
        [coords_ref[0], coords_ref[1], jnp.zeros((PACK - ROWS - 4, COLS), BF16)], axis=0
    )
    pack_ref[ROWS:, :] = rows_ref[...]
    total = None
    for leaf in range(2):
        for copy in copies[leaf]:
            copy.wait()
        part = jnp.dot(
            basis_buf[leaf], pack_ref[leaf * LEAF : (leaf + 1) * LEAF, :], preferred_element_type=F32
        )
        total = part if total is None else total + part
    s_ref[...] = total.astype(BF16)
    first.wait()
    order.wait()
    t_ref[0, 1] = folded(t_ref[0, 1], perm_ref[0:1, :])


def project(x, basis_t, coords, transfer, perm):
    return pl.pallas_call(
        project_kernel,
        out_shape=(
            jax.ShapeDtypeStruct((RANK, COLS), BF16),
            jax.ShapeDtypeStruct((PACK, COLS), BF16),
            jax.ShapeDtypeStruct((PACK - ROWS, COLS), BF16),
            jax.ShapeDtypeStruct((1, 2, RANK, RANK), BF16),
        ),
        in_specs=[HBM] * 5,
        out_specs=(VMEM,) * 4,
        scratch_shapes=[
            pltpu.VMEM((2, RANK, LEAF), BF16),
            pltpu.VMEM((2, 2, LEAF), BF16),
            pltpu.VMEM((LEVELS, RANK), jnp.int32),
            pltpu.SemaphoreType.DMA((7,)),
        ],
        compiler_params=params(),
        name="project",
    )(*(in_hbm(array) for array in (x, basis_t, coords, transfer, perm)))


def prepare_kernel(transfer_ref, perm_ref, expand_ref, after_ref, t_ref, e_ref):
    for level in range(1, LEVELS):
        t_ref[level - 1, 0] = transfer_ref[level, 0]
        t_ref[level - 1, 1] = folded(transfer_ref[level, 1], perm_ref[level : level + 1, :])
    for leaf in range(2):
        e_ref[leaf * LEAF : (leaf + 1) * LEAF, :] = expand_ref[leaf].T


def prepare(transfer, perm, expand_t, after):
    return pl.pallas_call(
        prepare_kernel,
        out_shape=(
            jax.ShapeDtypeStruct((LEVELS - 1, 2, RANK, RANK), BF16),
            jax.ShapeDtypeStruct((ROWS, RANK), BF16),
        ),
        in_specs=[VMEM, VMEM, VMEM, VMEM],
        out_specs=(VMEM, VMEM),
        compiler_params=params(),
        name="prepare",
    )(transfer, perm, expand_t, after)


def level_kernel(t_ref, own_ref, other_ref, s_ref):
    total = jnp.dot(t_ref[0, 0], own_ref[...], preferred_element_type=F32)
    total = total + jnp.dot(t_ref[0, 1], other_ref[...], preferred_element_type=F32)
    s_ref[...] = total.astype(BF16)


def gathered_kernel(high_ref, t_ref, own_ref, both_ref, s_ref):
    total = jnp.dot(t_ref[0, 0], own_ref[...], preferred_element_type=F32)
    total = total + jnp.dot(
        t_ref[0, 1], both_ref[1 - high_ref[0]], preferred_element_type=F32
    )
    s_ref[...] = total.astype(BF16)


def level_step(t, index, own, other, high=None, weight=4 * RANK * RANK * COLS):
    flat = pl.BlockSpec((RANK, COLS), lambda i: (0, 0))
    specs = [pl.BlockSpec((1, 2, RANK, RANK), lambda i: (index, 0, 0, 0)), flat]
    if high is None:
        body, specs, args = level_kernel, specs + [flat], (t, own, other)
    else:
        both = pl.BlockSpec((2, RANK, COLS), lambda i: (0, 0, 0))
        body, specs, args = gathered_kernel, [SMEM] + specs + [both], (high, t, own, other)
    return pl.pallas_call(
        body,
        grid=(1,),
        out_shape=jax.ShapeDtypeStruct((RANK, COLS), BF16),
        in_specs=specs,
        out_specs=flat,
        compiler_params=params(),
        cost_estimate=pl.CostEstimate(
            flops=weight, transcendentals=0, bytes_accessed=6 * RANK * COLS
        ),
        name=f"level_{index}",
    )(*args)


def scaled(rows):
    return rows.astype(F32) * (1.0 / FACTOR)


def add_tile(index_ref, near_ref, target, offset, source, leaf, columns, rows):
    block = pl.ds(target * LEAF, LEAF)
    used = (
        (index_ref[target, 0] == offset)
        | (index_ref[target, 1] == offset)
        | (index_ref[target, 2] == offset)
    )

    @pl.when(used)
    def _():
        dx = columns[:, 2 * target : 2 * target + 1] - rows[2 * leaf : 2 * leaf + 1, :]
        dy = columns[:, 2 * target + 1 : 2 * target + 2] - rows[2 * leaf + 1 : 2 * leaf + 2, :]
        tile = lax.rsqrt(dx * dx + dy * dy + SOFT / FACTOR**2).astype(BF16)
        near_ref[block, :] += jnp.dot(
            tile, source[leaf * LEAF : (leaf + 1) * LEAF, :], preferred_element_type=F32
        )


def own_kernel(index_ref, own_ref, rows_ref, after_ref, near_ref):
    near_ref[...] = jnp.zeros((ROWS, COLS), F32)
    rows = scaled(rows_ref[:8, :])
    columns = rows.T
    for target in range(2):
        for leaf in range(2):
            add_tile(index_ref, near_ref, target, leaf - target, own_ref, leaf, columns, rows)


def near_own(index, own, rows, after):
    return pl.pallas_call(
        own_kernel,
        out_shape=jax.ShapeDtypeStruct((ROWS, COLS), F32),
        in_specs=[SMEM, VMEM, VMEM, VMEM],
        out_specs=VMEM,
        compiler_params=params(),
        name="near_own",
    )(index, own, rows, after)


def sides_kernel(tests, index_ref, wide_ref, pair_ref, rows_ref, *refs):
    count = len(tests)
    sources = refs[:count]
    near_ref = refs[count + 1]
    bufs, sems = refs[count + 2 : -1], refs[-1]
    plan = []
    for i, test in enumerate(tests):
        low, high = test(wide_ref[0], pair_ref[0])
        copy = pltpu.make_async_copy(sources[i], bufs[i], sems.at[i])
        plan.append((low, high, copy, bufs[i]))

        @pl.when(low | high)
        def _(copy=copy):
            copy.start()

    for low, high, copy, buf in plan:

        @pl.when(low | high)
        def _(copy=copy):
            copy.wait()

        for shift, present in ((-2, low), (2, high)):

            @pl.when(present)
            def _(shift=shift, buf=buf):
                columns = scaled(rows_ref[:8, :]).T
                rows = scaled(buf[ROWS : ROWS + 8, :])
                for target in range(2):
                    for leaf in range(2):
                        offset = shift + leaf - target
                        if abs(offset) <= 2:
                            add_tile(index_ref, near_ref, target, offset, buf, leaf, columns, rows)


def near_sides(name, weight, index, place, rows, tests, sources, near):
    count = len(tests)
    return pl.pallas_call(
        functools.partial(sides_kernel, tests),
        out_shape=jax.ShapeDtypeStruct((ROWS, COLS), F32),
        in_specs=[SMEM] * 3 + [VMEM] + [ANY] * count + [VMEM],
        out_specs=VMEM,
        scratch_shapes=[pltpu.VMEM((PACK, COLS), BF16)] * count
        + [pltpu.SemaphoreType.DMA((count,))],
        input_output_aliases={4 + count: 0},
        compiler_params=params(),
        cost_estimate=pl.CostEstimate(
            flops=weight, transcendentals=0, bytes_accessed=ROWS * COLS * 8
        ),
        name=name,
    )(index, *place, rows, *sources, near)


def final_kernel(t_ref, own_ref, other_ref, e_ref, near_ref, out_ref, s_ref):
    @pl.when(pl.program_id(0) == 0)
    def _():
        total = jnp.dot(t_ref[0, 0], own_ref[...], preferred_element_type=F32)
        total = total + jnp.dot(t_ref[0, 1], other_ref[...], preferred_element_type=F32)
        s_ref[...] = total.astype(BF16)

    distant = jnp.dot(e_ref[...], s_ref[...], preferred_element_type=F32)
    out_ref[...] = (near_ref[...] + distant).astype(BF16)


def final_step(t, own, other, e, near):
    block = 256
    return pl.pallas_call(
        final_kernel,
        grid=(ROWS // block,),
        out_shape=jax.ShapeDtypeStruct((ROWS, COLS), BF16),
        in_specs=[
            pl.BlockSpec((1, 2, RANK, RANK), lambda i: (LEVELS - 2, 0, 0, 0)),
            pl.BlockSpec((RANK, COLS), lambda i: (0, 0)),
            pl.BlockSpec((RANK, COLS), lambda i: (0, 0)),
            pl.BlockSpec((block, RANK), lambda i: (i, 0)),
            pl.BlockSpec((block, COLS), lambda i: (i, 0)),
        ],
        out_specs=pl.BlockSpec((block, COLS), lambda i: (i, 0)),
        scratch_shapes=[pltpu.VMEM((RANK, COLS), BF16)],
        compiler_params=params(),
        name="final",
    )(t, own, other, e, near)


def from_partner(block, axis, bit):
    count = lax.axis_size(axis)
    return lax.ppermute(block, axis, [(i, i ^ (1 << bit)) for i in range(count)])


def with_partner(block, axis, bit):
    count = lax.axis_size(axis)
    pairs = [[i, i | 1 << bit] for i in range(count) if not i >> bit & 1]
    both = lax.all_gather(block, axis, axis_index_groups=pairs)
    high = (lax.axis_index(axis) >> bit & 1).reshape(1)
    return both, high


def on_device(rhs, coords, near_index, project_basis, expand_basis, transfer, level_perm):
    axes = ("wide", "pair")
    wide, pair = lax.axis_size("wide"), lax.axis_size("pair")
    devices = wide * pair
    turn = 4 * pair

    def odd(i):
        return i % 2 == 1

    def even(i):
        return (i % 2 == 0) & (i % RUN != 0)

    def outer(i):
        return (i % RUN == 0) & (i % turn != 0)

    def far(i):
        return i % turn == 0

    def swapped(block, keep):
        up = [(i - 1, i) for i in range(1, devices) if keep(i)]
        return lax.ppermute(block, axes, up + [(b, a) for a, b in up])

    def met(keep):
        def test(w, q):
            i = w * pair + q
            return keep(i) & (i > 0), keep(i + 1) & (i + 1 < devices)

        return test

    place = (lax.axis_index("wide").reshape(1), lax.axis_index("pair").reshape(1))
    s, pack, rows, t0 = project(
        rhs, jnp.swapaxes(project_basis, 1, 2), coords, transfer[0], level_perm
    )
    odd_side = swapped(pack, odd)
    even_side = swapped(pack, even)
    both, high_bit = with_partner(s, "wide", 0)
    s = level_step(t0, 0, s, both, high_bit)
    partner = from_partner(s, "wide", 1)
    t, e = prepare(transfer[0], level_perm, jnp.swapaxes(expand_basis, 1, 2), s)
    sent, e = lax.optimization_barrier((pack, e))
    outer_side = swapped(sent, outer)
    s = level_step(t, 0, s, partner, weight=COVER_1)
    partner = from_partner(s, "wide", 2)
    sent, s = lax.optimization_barrier((sent, s))
    far_side = swapped(sent, far)
    near = near_own(near_index, sent, rows, s)
    partner, near = lax.optimization_barrier((partner, near))
    s = level_step(t, 1, s, partner)
    both, high_bit = with_partner(s, "pair", 0)
    s = level_step(t, 2, s, both, high_bit)
    partner = from_partner(s, "pair", 1)

    def add(name, weight, near, *sides):
        tests = [met(keep) for keep, _ in sides]
        sources = [side for _, side in sides]
        return near_sides(name, weight, near_index, place, rows, tests, sources, near)

    near = add(
        "near_inner", COVER_INNER, near, (odd, in_hbm(odd_side)), (even, in_hbm(even_side))
    )
    near = add("near_outer", COVER_OUTER, near, (outer, outer_side))
    near = add("near_far", COVER_FAR, near, (far, far_side))
    return final_step(t, s, partner, e, near)


def solution(mesh):
    return jax.shard_map(
        on_device,
        mesh=mesh,
        in_specs=(
            P(("wide", "pair"), None),
            P(("wide", "pair"), None, None),
            P(("wide", "pair"), None),
            P(("wide", "pair"), None, None),
            P(("wide", "pair"), None, None),
            P(("wide", "pair"), None, None, None, None),
            P(),
        ),
        out_specs=P(("wide", "pair"), None),
        check_vma=False,
    )
```

```python
import functools
import math

import jax
import jax.numpy as jnp
from jax import lax
from jax.experimental import pallas as pl
from jax.experimental.pallas import tpu as pltpu
from jax.sharding import PartitionSpec as P

LW = 3
LP = 2
LEVELS = LW + LP
LEAF = 512
RANK = 192
COLS = 512
ROWS = 1024
PACK = ROWS + 16
RUN = 8
CHUNK = 128
PIECE = 128
COVER_1 = 3_000_000_000
COVER_ODD = 3_500_000_000
COVER_EVEN = 1_000_000_000
COVER_OUTER = 6_000_000_000
COVER_FAR = 4_000_000_000
SOFT = 0.0004
FACTOR = 0.25 / math.sqrt(LEAF)
F32 = jnp.float32
BF16 = jnp.bfloat16
VMEM = pl.BlockSpec(memory_space=pltpu.VMEM)
HBM = pl.BlockSpec(memory_space=pltpu.HBM)
ANY = pl.BlockSpec(memory_space=pl.ANY)
SMEM = pl.BlockSpec(memory_space=pltpu.SMEM)


def in_hbm(array):
    return pltpu.with_memory_space_constraint(array, pltpu.HBM)


def params():
    return pltpu.CompilerParams(vmem_limit_bytes=16 << 20)


def folded(matrix, perm_row):
    k = lax.broadcasted_iota(jnp.int32, (RANK, RANK), 0)
    picked = jnp.where(k == perm_row, 1.0, 0.0).astype(BF16)
    return lax.dot_general(
        matrix, picked, (((1,), (1,)), ((), ())), preferred_element_type=F32
    ).astype(BF16)


def project_kernel(
    x_ref,
    basis_ref,
    points_ref,
    transfer_ref,
    order_ref,
    s_ref,
    pack_ref,
    rows_ref,
    t_ref,
    basis_buf,
    coords_ref,
    perm_ref,
    sems,
):
    points = pltpu.make_async_copy(points_ref, coords_ref, sems.at[0])
    first = pltpu.make_async_copy(transfer_ref.at[0], t_ref.at[0], sems.at[1])
    order = pltpu.make_async_copy(order_ref, perm_ref, sems.at[2])
    copies = []
    for leaf in range(2):
        block = pl.ds(leaf * LEAF, LEAF)
        copies.append(
            (
                pltpu.make_async_copy(basis_ref.at[leaf], basis_buf.at[leaf], sems.at[3 + leaf]),
                pltpu.make_async_copy(x_ref.at[block], pack_ref.at[block], sems.at[5 + leaf]),
            )
        )
    points.start()
    for pair in copies:
        for copy in pair:
            copy.start()
    first.start()
    order.start()
    points.wait()
    rows_ref[...] = jnp.concatenate(
        [coords_ref[0], coords_ref[1], jnp.zeros((PACK - ROWS - 4, COLS), BF16)], axis=0
    )
    pack_ref[ROWS:, :] = rows_ref[...]
    total = None
    for leaf in range(2):
        for copy in copies[leaf]:
            copy.wait()
        part = jnp.dot(
            basis_buf[leaf], pack_ref[leaf * LEAF : (leaf + 1) * LEAF, :], preferred_element_type=F32
        )
        total = part if total is None else total + part
    s_ref[...] = total.astype(BF16)
    first.wait()
    order.wait()
    t_ref[0, 1] = folded(t_ref[0, 1], perm_ref[0:1, :])


def project(x, basis_t, coords, transfer, perm):
    return pl.pallas_call(
        project_kernel,
        out_shape=(
            jax.ShapeDtypeStruct((RANK, COLS), BF16),
            jax.ShapeDtypeStruct((PACK, COLS), BF16),
            jax.ShapeDtypeStruct((PACK - ROWS, COLS), BF16),
            jax.ShapeDtypeStruct((1, 2, RANK, RANK), BF16),
        ),
        in_specs=[HBM] * 5,
        out_specs=(VMEM,) * 4,
        scratch_shapes=[
            pltpu.VMEM((2, RANK, LEAF), BF16),
            pltpu.VMEM((2, 2, LEAF), BF16),
            pltpu.VMEM((LEVELS, RANK), jnp.int32),
            pltpu.SemaphoreType.DMA((7,)),
        ],
        compiler_params=params(),
        name="project",
    )(*(in_hbm(array) for array in (x, basis_t, coords, transfer, perm)))


def prepare_kernel(transfer_ref, perm_ref, after_ref, t_ref):
    for level in range(1, LEVELS):
        t_ref[level - 1, 0] = transfer_ref[level, 0]
        t_ref[level - 1, 1] = folded(transfer_ref[level, 1], perm_ref[level : level + 1, :])


def prepare(transfer, perm, after):
    return pl.pallas_call(
        prepare_kernel,
        out_shape=jax.ShapeDtypeStruct((LEVELS - 1, 2, RANK, RANK), BF16),
        in_specs=[VMEM, VMEM, VMEM],
        out_specs=VMEM,
        compiler_params=params(),
        name="prepare",
    )(transfer, perm, after)


def level_kernel(t_ref, own_ref, other_ref, s_ref):
    total = jnp.dot(t_ref[0, 0], own_ref[...], preferred_element_type=F32)
    total = total + jnp.dot(t_ref[0, 1], other_ref[...], preferred_element_type=F32)
    s_ref[...] = total.astype(BF16)


def gathered_kernel(high_ref, t_ref, own_ref, both_ref, s_ref):
    total = jnp.dot(t_ref[0, 0], own_ref[...], preferred_element_type=F32)
    total = total + jnp.dot(
        t_ref[0, 1], both_ref[1 - high_ref[0]], preferred_element_type=F32
    )
    s_ref[...] = total.astype(BF16)


def level_step(t, index, own, other, high=None, weight=4 * RANK * RANK * COLS):
    flat = pl.BlockSpec((RANK, COLS), lambda i: (0, 0))
    specs = [pl.BlockSpec((1, 2, RANK, RANK), lambda i: (index, 0, 0, 0)), flat]
    if high is None:
        body, specs, args = level_kernel, specs + [flat], (t, own, other)
    else:
        both = pl.BlockSpec((2, RANK, COLS), lambda i: (0, 0, 0))
        body, specs, args = gathered_kernel, [SMEM] + specs + [both], (high, t, own, other)
    return pl.pallas_call(
        body,
        grid=(1,),
        out_shape=jax.ShapeDtypeStruct((RANK, COLS), BF16),
        in_specs=specs,
        out_specs=flat,
        compiler_params=params(),
        cost_estimate=pl.CostEstimate(
            flops=weight, transcendentals=0, bytes_accessed=6 * RANK * COLS
        ),
        name=f"level_{index}",
    )(*args)


def scaled(rows):
    return rows.astype(F32) * (1.0 / FACTOR)


def add_tile(index_ref, near_ref, target, offset, source, leaf, columns, rows):
    used = (
        (index_ref[target, 0] == offset)
        | (index_ref[target, 1] == offset)
        | (index_ref[target, 2] == offset)
    )

    @pl.when(used)
    def _():
        sx = rows[2 * leaf : 2 * leaf + 1, :]
        sy = rows[2 * leaf + 1 : 2 * leaf + 2, :]
        held = source[leaf * LEAF : (leaf + 1) * LEAF, :]
        for start in range(0, LEAF, PIECE):
            part = columns[start : start + PIECE]
            dx = part[:, 2 * target : 2 * target + 1] - sx
            dy = part[:, 2 * target + 1 : 2 * target + 2] - sy
            tile = lax.rsqrt(dx * dx + dy * dy + SOFT / FACTOR**2).astype(BF16)
            near_ref[pl.ds(target * LEAF + start, PIECE), :] += jnp.dot(
                tile, held, preferred_element_type=F32
            )


def own_kernel(index_ref, own_ref, rows_ref, expand_ref, after_ref, near_ref, e_ref):
    for leaf in range(2):
        e_ref[leaf * LEAF : (leaf + 1) * LEAF, :] = expand_ref[leaf].T
    near_ref[...] = jnp.zeros((ROWS, COLS), F32)
    rows = scaled(rows_ref[:8, :])
    columns = rows.T
    for target in range(2):
        for leaf in range(2):
            add_tile(index_ref, near_ref, target, leaf - target, own_ref, leaf, columns, rows)


def near_own(index, own, rows, expand_t, after):
    return pl.pallas_call(
        own_kernel,
        out_shape=(
            jax.ShapeDtypeStruct((ROWS, COLS), F32),
            jax.ShapeDtypeStruct((ROWS, RANK), BF16),
        ),
        in_specs=[SMEM] + [VMEM] * 4,
        out_specs=(VMEM, VMEM),
        compiler_params=params(),
        name="near_own",
    )(index, own, rows, expand_t, after)


def side_kernel(
    test, index_ref, wide_ref, pair_ref, rows_ref, source_ref, _, near_ref, buf, sems
):
    low, high = test(wide_ref[0], pair_ref[0])
    spans = ((ROWS, PACK - ROWS), (0, LEAF), (LEAF, LEAF))
    copies = []
    for i, (start, size) in enumerate(spans):
        block = pl.ds(start, size)
        copies.append(pltpu.make_async_copy(source_ref.at[block], buf.at[block], sems.at[i]))

    @pl.when(low | high)
    def _():
        for copy in copies:
            copy.start()

    for shift, present in ((-2, low), (2, high)):

        @pl.when(present)
        def _(shift=shift):
            copies[0].wait()
            columns = scaled(rows_ref[:8, :]).T
            rows = scaled(buf[ROWS : ROWS + 8, :])
            for leaf in range(2):
                copies[1 + leaf].wait()
                for target in range(2):
                    offset = shift + leaf - target
                    if abs(offset) <= 2:
                        add_tile(index_ref, near_ref, target, offset, buf, leaf, columns, rows)


def near_side(name, weight, index, place, rows, test, source, near):
    return pl.pallas_call(
        functools.partial(side_kernel, test),
        out_shape=jax.ShapeDtypeStruct((ROWS, COLS), F32),
        in_specs=[SMEM] * 3 + [VMEM, ANY, VMEM],
        out_specs=VMEM,
        scratch_shapes=[pltpu.VMEM((PACK, COLS), BF16), pltpu.SemaphoreType.DMA((3,))],
        input_output_aliases={5: 0},
        compiler_params=params(),
        cost_estimate=pl.CostEstimate(
            flops=weight, transcendentals=0, bytes_accessed=ROWS * COLS * 8
        ),
        name=name,
    )(index, *place, rows, source, near)


def final_kernel(t_ref, own_ref, other_ref, e_ref, near_ref, out_ref, out_buf, sems):
    total = jnp.dot(t_ref[LEVELS - 2, 0], own_ref[...], preferred_element_type=F32)
    total = total + jnp.dot(t_ref[LEVELS - 2, 1], other_ref[...], preferred_element_type=F32)
    s = total.astype(BF16)
    copies = []
    for i in range(ROWS // CHUNK):
        block = pl.ds(i * CHUNK, CHUNK)
        distant = jnp.dot(e_ref[block, :], s, preferred_element_type=F32)
        out_buf[block, :] = (near_ref[block, :] + distant).astype(BF16)
        copies.append(pltpu.make_async_copy(out_buf.at[block], out_ref.at[block], sems.at[i]))
        copies[-1].start()
    for copy in copies:
        copy.wait()


def final_step(t, own, other, e, near):
    return pl.pallas_call(
        final_kernel,
        out_shape=jax.ShapeDtypeStruct((ROWS, COLS), BF16),
        in_specs=[VMEM] * 5,
        out_specs=HBM,
        scratch_shapes=[
            pltpu.VMEM((ROWS, COLS), BF16),
            pltpu.SemaphoreType.DMA((ROWS // CHUNK,)),
        ],
        compiler_params=params(),
        name="final",
    )(t, own, other, e, near)


def from_partner(block, axis, bit):
    count = lax.axis_size(axis)
    return lax.ppermute(block, axis, [(i, i ^ (1 << bit)) for i in range(count)])


def with_partner(block, axis, bit):
    count = lax.axis_size(axis)
    pairs = [[i, i | 1 << bit] for i in range(count) if not i >> bit & 1]
    both = lax.all_gather(block, axis, axis_index_groups=pairs)
    high = (lax.axis_index(axis) >> bit & 1).reshape(1)
    return both, high


def on_device(rhs, coords, near_index, project_basis, expand_basis, transfer, level_perm):
    axes = ("wide", "pair")
    wide, pair = lax.axis_size("wide"), lax.axis_size("pair")
    devices = wide * pair
    turn = 4 * pair

    def odd(i):
        return i % 2 == 1

    def even(i):
        return (i % 2 == 0) & (i % RUN != 0)

    def outer(i):
        return (i % RUN == 0) & (i % turn != 0)

    def far(i):
        return i % turn == 0

    def swapped(block, keep):
        up = [(i - 1, i) for i in range(1, devices) if keep(i)]
        return lax.ppermute(block, axes, up + [(b, a) for a, b in up])

    def met(keep):
        def test(w, q):
            i = w * pair + q
            return keep(i) & (i > 0), keep(i + 1) & (i + 1 < devices)

        return test

    place = (lax.axis_index("wide").reshape(1), lax.axis_index("pair").reshape(1))
    s, pack, rows, t0 = project(
        rhs, jnp.swapaxes(project_basis, 1, 2), coords, transfer[0], level_perm
    )
    odd_side = swapped(pack, odd)
    both, high_bit = with_partner(s, "wide", 0)
    s = level_step(t0, 0, s, both, high_bit)
    partner = from_partner(s, "wide", 1)
    sent, s = lax.optimization_barrier((pack, s))
    outer_side = swapped(sent, outer)
    even_side = swapped(sent, even)
    t = prepare(transfer[0], level_perm, s)
    s = level_step(t, 0, s, partner, weight=COVER_1)
    partner = from_partner(s, "wide", 2)
    sent, s = lax.optimization_barrier((sent, s))
    far_side = swapped(sent, far)
    near, e = near_own(near_index, sent, rows, jnp.swapaxes(expand_basis, 1, 2), s)
    partner, near = lax.optimization_barrier((partner, near))
    s = level_step(t, 1, s, partner)
    both, high_bit = with_partner(s, "pair", 0)
    s = level_step(t, 2, s, both, high_bit)
    partner = from_partner(s, "pair", 1)

    for name, weight, keep, side in (
        ("near_odd", COVER_ODD, odd, in_hbm(odd_side)),
        ("near_even", COVER_EVEN, even, in_hbm(even_side)),
        ("near_outer", COVER_OUTER, outer, in_hbm(outer_side)),
        ("near_far", COVER_FAR, far, far_side),
    ):
        near = near_side(name, weight, near_index, place, rows, met(keep), side, near)
    return final_step(t, s, partner, e, near)


def solution(mesh):
    return jax.shard_map(
        on_device,
        mesh=mesh,
        in_specs=(
            P(("wide", "pair"), None),
            P(("wide", "pair"), None, None),
            P(("wide", "pair"), None),
            P(("wide", "pair"), None, None),
            P(("wide", "pair"), None, None),
            P(("wide", "pair"), None, None, None, None),
            P(),
        ),
        out_specs=P(("wide", "pair"), None),
        check_vma=False,
    )
```

```python
import functools
import math

import jax
import jax.numpy as jnp
from jax import lax
from jax.experimental import pallas as pl
from jax.experimental.pallas import tpu as pltpu
from jax.sharding import PartitionSpec as P

LW = 3
LP = 2
LEVELS = LW + LP
LEAF = 512
RANK = 192
COLS = 512
ROWS = 1024
PACK = ROWS + 16
RUN = 8
CHUNK = 128
PIECE = 128
COVER_1 = 3_000_000_000
COVER_ODD = 3_500_000_000
COVER_EVEN = 1_000_000_000
COVER_OUTER = 6_000_000_000
COVER_FAR = 4_000_000_000
SOFT = 0.0004
FACTOR = 0.25 / math.sqrt(LEAF)
F32 = jnp.float32
BF16 = jnp.bfloat16
VMEM = pl.BlockSpec(memory_space=pltpu.VMEM)
HBM = pl.BlockSpec(memory_space=pltpu.HBM)
ANY = pl.BlockSpec(memory_space=pl.ANY)
SMEM = pl.BlockSpec(memory_space=pltpu.SMEM)


def in_hbm(array):
    return pltpu.with_memory_space_constraint(array, pltpu.HBM)


def params():
    return pltpu.CompilerParams(vmem_limit_bytes=16 << 20)


def folded(matrix, perm_row):
    k = lax.broadcasted_iota(jnp.int32, (RANK, RANK), 0)
    picked = jnp.where(k == perm_row, 1.0, 0.0).astype(BF16)
    return lax.dot_general(
        matrix, picked, (((1,), (1,)), ((), ())), preferred_element_type=F32
    ).astype(BF16)


def project_kernel(
    x_ref,
    basis_ref,
    points_ref,
    transfer_ref,
    order_ref,
    s_ref,
    pack_ref,
    rows_ref,
    t_ref,
    basis_buf,
    coords_ref,
    perm_ref,
    sems,
):
    points = pltpu.make_async_copy(points_ref, coords_ref, sems.at[0])
    first = pltpu.make_async_copy(transfer_ref.at[0], t_ref.at[0], sems.at[1])
    order = pltpu.make_async_copy(order_ref, perm_ref, sems.at[2])
    copies = []
    for leaf in range(2):
        block = pl.ds(leaf * LEAF, LEAF)
        copies.append(
            (
                pltpu.make_async_copy(basis_ref.at[leaf], basis_buf.at[leaf], sems.at[3 + leaf]),
                pltpu.make_async_copy(x_ref.at[block], pack_ref.at[block], sems.at[5 + leaf]),
            )
        )
    points.start()
    for pair in copies:
        for copy in pair:
            copy.start()
    first.start()
    order.start()
    points.wait()
    rows_ref[...] = jnp.concatenate(
        [coords_ref[0], coords_ref[1], jnp.zeros((PACK - ROWS - 4, COLS), BF16)], axis=0
    )
    pack_ref[ROWS:, :] = rows_ref[...]
    total = None
    for leaf in range(2):
        for copy in copies[leaf]:
            copy.wait()
        part = jnp.dot(
            basis_buf[leaf], pack_ref[leaf * LEAF : (leaf + 1) * LEAF, :], preferred_element_type=F32
        )
        total = part if total is None else total + part
    s_ref[...] = total.astype(BF16)
    first.wait()
    order.wait()
    t_ref[0, 1] = folded(t_ref[0, 1], perm_ref[0:1, :])


def project(x, basis_t, coords, transfer, perm):
    return pl.pallas_call(
        project_kernel,
        out_shape=(
            jax.ShapeDtypeStruct((RANK, COLS), BF16),
            jax.ShapeDtypeStruct((PACK, COLS), BF16),
            jax.ShapeDtypeStruct((PACK - ROWS, COLS), BF16),
            jax.ShapeDtypeStruct((1, 2, RANK, RANK), BF16),
        ),
        in_specs=[HBM] * 5,
        out_specs=(VMEM,) * 4,
        scratch_shapes=[
            pltpu.VMEM((2, RANK, LEAF), BF16),
            pltpu.VMEM((2, 2, LEAF), BF16),
            pltpu.VMEM((LEVELS, RANK), jnp.int32),
            pltpu.SemaphoreType.DMA((7,)),
        ],
        compiler_params=params(),
        name="project",
    )(*(in_hbm(array) for array in (x, basis_t, coords, transfer, perm)))


def prepare_kernel(transfer_ref, perm_ref, after_ref, t_ref):
    t_ref[0, 0] = transfer_ref[1, 0]
    t_ref[0, 1] = folded(transfer_ref[1, 1], perm_ref[1:2, :])


def prepare(transfer, perm, after):
    return pl.pallas_call(
        prepare_kernel,
        out_shape=jax.ShapeDtypeStruct((1, 2, RANK, RANK), BF16),
        in_specs=[VMEM, VMEM, VMEM],
        out_specs=VMEM,
        compiler_params=params(),
        name="prepare",
    )(transfer, perm, after)


def level_kernel(t_ref, own_ref, other_ref, s_ref):
    total = jnp.dot(t_ref[0, 0], own_ref[...], preferred_element_type=F32)
    total = total + jnp.dot(t_ref[0, 1], other_ref[...], preferred_element_type=F32)
    s_ref[...] = total.astype(BF16)


def gathered_kernel(high_ref, t_ref, own_ref, both_ref, s_ref):
    total = jnp.dot(t_ref[0, 0], own_ref[...], preferred_element_type=F32)
    total = total + jnp.dot(
        t_ref[0, 1], both_ref[1 - high_ref[0]], preferred_element_type=F32
    )
    s_ref[...] = total.astype(BF16)


def level_step(t, index, own, other, high=None, weight=4 * RANK * RANK * COLS):
    flat = pl.BlockSpec((RANK, COLS), lambda i: (0, 0))
    specs = [pl.BlockSpec((1, 2, RANK, RANK), lambda i: (index, 0, 0, 0)), flat]
    if high is None:
        body, specs, args = level_kernel, specs + [flat], (t, own, other)
    else:
        both = pl.BlockSpec((2, RANK, COLS), lambda i: (0, 0, 0))
        body, specs, args = gathered_kernel, [SMEM] + specs + [both], (high, t, own, other)
    return pl.pallas_call(
        body,
        grid=(1,),
        out_shape=jax.ShapeDtypeStruct((RANK, COLS), BF16),
        in_specs=specs,
        out_specs=flat,
        compiler_params=params(),
        cost_estimate=pl.CostEstimate(
            flops=weight, transcendentals=0, bytes_accessed=6 * RANK * COLS
        ),
        name=f"level_{index}",
    )(*args)


def scaled(rows):
    return rows.astype(F32) * (1.0 / FACTOR)


def wanted(index_ref, target, offset):
    return (
        (index_ref[target, 0] == offset)
        | (index_ref[target, 1] == offset)
        | (index_ref[target, 2] == offset)
    )


def tile_of(columns, rows, target, leaf):
    dx = columns[:, 2 * target : 2 * target + 1] - rows[2 * leaf : 2 * leaf + 1, :]
    dy = columns[:, 2 * target + 1 : 2 * target + 2] - rows[2 * leaf + 1 : 2 * leaf + 2, :]
    return lax.rsqrt(dx * dx + dy * dy + SOFT / FACTOR**2).astype(BF16)


def add_tile(index_ref, near_ref, target, offset, source, leaf, columns, rows):
    @pl.when(wanted(index_ref, target, offset))
    def _():
        held = source[leaf * LEAF : (leaf + 1) * LEAF, :]
        for start in range(0, LEAF, PIECE):
            tile = tile_of(columns[start : start + PIECE], rows, target, leaf)
            near_ref[pl.ds(target * LEAF + start, PIECE), :] += jnp.dot(
                tile, held, preferred_element_type=F32
            )


def own_kernel(
    index_ref, own_ref, rows_ref, expand_ref, transfer_ref, perm_ref, _, near_ref, e_ref, t_ref
):
    for level in range(2, LEVELS):
        t_ref[level - 2, 0] = transfer_ref[level, 0]
        t_ref[level - 2, 1] = folded(transfer_ref[level, 1], perm_ref[level : level + 1, :])
    for leaf in range(2):
        e_ref[leaf * LEAF : (leaf + 1) * LEAF, :] = expand_ref[leaf].T
    near_ref[...] = jnp.zeros((ROWS, COLS), F32)
    rows = scaled(rows_ref[:8, :])
    columns = rows.T
    for target in range(2):
        for leaf in range(2):
            add_tile(index_ref, near_ref, target, leaf - target, own_ref, leaf, columns, rows)


def near_own(index, own, rows, expand_t, transfer, perm, after):
    return pl.pallas_call(
        own_kernel,
        out_shape=(
            jax.ShapeDtypeStruct((ROWS, COLS), F32),
            jax.ShapeDtypeStruct((ROWS, RANK), BF16),
            jax.ShapeDtypeStruct((LEVELS - 2, 2, RANK, RANK), BF16),
        ),
        in_specs=[SMEM] + [VMEM] * 6,
        out_specs=(VMEM,) * 3,
        compiler_params=params(),
        name="near_own",
    )(index, own, rows, expand_t, transfer, perm, after)


def side_kernel(
    test, table_ref, rows_ref, source_ref, _, near_ref, buf, tiles, index_ref, sems
):
    low, high = test(lax.axis_index("wide"), lax.axis_index("pair"))
    spans = ((ROWS, PACK - ROWS), (0, LEAF), (LEAF, LEAF))
    copies = []
    for i, (start, size) in enumerate(spans):
        block = pl.ds(start, size)
        copies.append(pltpu.make_async_copy(source_ref.at[block], buf.at[block], sems.at[i]))
    table = pltpu.make_async_copy(table_ref, index_ref, sems.at[3])

    @pl.when(low | high)
    def _():
        table.start()
        for copy in copies:
            copy.start()

    for shift, present in ((-2, low), (2, high)):

        @pl.when(present)
        def _(shift=shift):
            pairs = [
                (leaf, target, shift + leaf - target)
                for leaf in range(2)
                for target in range(2)
                if abs(shift + leaf - target) <= 2
            ]
            table.wait()
            copies[0].wait()
            columns = scaled(rows_ref[:8, :]).T
            rows = scaled(buf[ROWS : ROWS + 8, :])
            for i, (leaf, target, offset) in enumerate(pairs):

                @pl.when(wanted(index_ref, target, offset))
                def _(i=i, leaf=leaf, target=target):
                    for start in range(0, LEAF, PIECE):
                        tiles[i, start : start + PIECE, :] = tile_of(
                            columns[start : start + PIECE], rows, target, leaf
                        )

            for copy in copies[1:]:
                copy.wait()
            for i, (leaf, target, offset) in enumerate(pairs):

                @pl.when(wanted(index_ref, target, offset))
                def _(i=i, leaf=leaf, target=target):
                    near_ref[target * LEAF : (target + 1) * LEAF, :] += jnp.dot(
                        tiles[i],
                        buf[leaf * LEAF : (leaf + 1) * LEAF, :],
                        preferred_element_type=F32,
                    )


def near_side(name, weight, index, rows, test, source, near):
    return pl.pallas_call(
        functools.partial(side_kernel, test),
        out_shape=jax.ShapeDtypeStruct((ROWS, COLS), F32),
        in_specs=[HBM, VMEM, ANY, VMEM],
        out_specs=VMEM,
        scratch_shapes=[
            pltpu.VMEM((PACK, COLS), BF16),
            pltpu.VMEM((3, LEAF, LEAF), BF16),
            pltpu.SMEM((2, 3), jnp.int32),
            pltpu.SemaphoreType.DMA((4,)),
        ],
        input_output_aliases={3: 0},
        compiler_params=params(),
        cost_estimate=pl.CostEstimate(
            flops=weight, transcendentals=0, bytes_accessed=ROWS * COLS * 8
        ),
        name=name,
    )(in_hbm(index), rows, source, near)


def final_kernel(t_ref, own_ref, other_ref, e_ref, near_ref, out_ref, out_buf, sems):
    total = jnp.dot(t_ref[LEVELS - 3, 0], own_ref[...], preferred_element_type=F32)
    total = total + jnp.dot(t_ref[LEVELS - 3, 1], other_ref[...], preferred_element_type=F32)
    s = total.astype(BF16)
    copies = []
    for i in range(ROWS // CHUNK):
        block = pl.ds(i * CHUNK, CHUNK)
        distant = jnp.dot(e_ref[block, :], s, preferred_element_type=F32)
        out_buf[block, :] = (near_ref[block, :] + distant).astype(BF16)
        copies.append(pltpu.make_async_copy(out_buf.at[block], out_ref.at[block], sems.at[i]))
        copies[-1].start()
    for copy in copies:
        copy.wait()


def final_step(t, own, other, e, near):
    return pl.pallas_call(
        final_kernel,
        out_shape=jax.ShapeDtypeStruct((ROWS, COLS), BF16),
        in_specs=[VMEM] * 5,
        out_specs=HBM,
        scratch_shapes=[
            pltpu.VMEM((ROWS, COLS), BF16),
            pltpu.SemaphoreType.DMA((ROWS // CHUNK,)),
        ],
        compiler_params=params(),
        name="final",
    )(t, own, other, e, near)


def from_partner(block, axis, bit):
    count = lax.axis_size(axis)
    return lax.ppermute(block, axis, [(i, i ^ (1 << bit)) for i in range(count)])


def with_partner(block, axis, bit):
    count = lax.axis_size(axis)
    pairs = [[i, i | 1 << bit] for i in range(count) if not i >> bit & 1]
    both = lax.all_gather(block, axis, axis_index_groups=pairs)
    high = (lax.axis_index(axis) >> bit & 1).reshape(1)
    return both, high


def on_device(rhs, coords, near_index, project_basis, expand_basis, transfer, level_perm):
    axes = ("wide", "pair")
    wide, pair = lax.axis_size("wide"), lax.axis_size("pair")
    devices = wide * pair
    turn = 4 * pair

    def odd(i):
        return i % 2 == 1

    def even(i):
        return (i % 2 == 0) & (i % RUN != 0)

    def outer(i):
        return (i % RUN == 0) & (i % turn != 0)

    def far(i):
        return i % turn == 0

    def swapped(block, keep):
        up = [(i - 1, i) for i in range(1, devices) if keep(i)]
        return lax.ppermute(block, axes, up + [(b, a) for a, b in up])

    def met(keep):
        def test(w, q):
            i = w * pair + q
            return keep(i) & (i > 0), keep(i + 1) & (i + 1 < devices)

        return test

    s, pack, rows, t0 = project(
        rhs, jnp.swapaxes(project_basis, 1, 2), coords, transfer[0], level_perm
    )
    odd_side = swapped(pack, odd)
    both, high_bit = with_partner(s, "wide", 0)
    s = level_step(t0, 0, s, both, high_bit)
    partner = from_partner(s, "wide", 1)
    sent, s = lax.optimization_barrier((pack, s))
    outer_side = swapped(sent, outer)
    even_side = swapped(sent, even)
    t1 = prepare(transfer[0], level_perm, s)
    s = level_step(t1, 0, s, partner, weight=COVER_1)
    partner = from_partner(s, "wide", 2)
    sent, s = lax.optimization_barrier((sent, s))
    far_side = swapped(sent, far)
    near, e, t = near_own(
        near_index, sent, rows, jnp.swapaxes(expand_basis, 1, 2), transfer[0], level_perm, s
    )
    partner, near = lax.optimization_barrier((partner, near))
    s = level_step(t, 0, s, partner)
    both, high_bit = with_partner(s, "pair", 0)
    s = level_step(t, 1, s, both, high_bit)
    partner = from_partner(s, "pair", 1)

    for name, weight, keep, side in (
        ("near_odd", COVER_ODD, odd, in_hbm(odd_side)),
        ("near_even", COVER_EVEN, even, in_hbm(even_side)),
        ("near_outer", COVER_OUTER, outer, in_hbm(outer_side)),
        ("near_far", COVER_FAR, far, far_side),
    ):
        near = near_side(name, weight, near_index, rows, met(keep), side, near)
    return final_step(t, s, partner, e, near)


def solution(mesh):
    return jax.shard_map(
        on_device,
        mesh=mesh,
        in_specs=(
            P(("wide", "pair"), None),
            P(("wide", "pair"), None, None),
            P(("wide", "pair"), None),
            P(("wide", "pair"), None, None),
            P(("wide", "pair"), None, None),
            P(("wide", "pair"), None, None, None, None),
            P(),
        ),
        out_specs=P(("wide", "pair"), None),
        check_vma=False,
    )
```

```python
import functools
import math

import jax
import jax.numpy as jnp
from jax import lax
from jax.experimental import pallas as pl
from jax.experimental.pallas import tpu as pltpu
from jax.sharding import PartitionSpec as P

LW = 3
LP = 2
LEVELS = LW + LP
LEAF = 512
RANK = 192
COLS = 512
ROWS = 1024
PACK = ROWS + 16
RUN = 8
CHUNK = 256
PIECE = 128
COVER_1 = 3_000_000_000
COVER_ODD = 3_500_000_000
COVER_EVEN = 1_000_000_000
COVER_OUTER = 6_000_000_000
COVER_FAR = 4_000_000_000
SOFT = 0.0004
FACTOR = 0.25 / math.sqrt(LEAF)
F32 = jnp.float32
BF16 = jnp.bfloat16
VMEM = pl.BlockSpec(memory_space=pltpu.VMEM)
HBM = pl.BlockSpec(memory_space=pltpu.HBM)
ANY = pl.BlockSpec(memory_space=pl.ANY)
SMEM = pl.BlockSpec(memory_space=pltpu.SMEM)


def in_hbm(array):
    return pltpu.with_memory_space_constraint(array, pltpu.HBM)


def params():
    return pltpu.CompilerParams(vmem_limit_bytes=16 << 20)


def folded(matrix, perm_row):
    k = lax.broadcasted_iota(jnp.int32, (RANK, RANK), 0)
    picked = jnp.where(k == perm_row, 1.0, 0.0).astype(BF16)
    return lax.dot_general(
        matrix, picked, (((1,), (1,)), ((), ())), preferred_element_type=F32
    ).astype(BF16)


def project_kernel(
    x_ref,
    basis_ref,
    points_ref,
    transfer_ref,
    order_ref,
    s_ref,
    pack_ref,
    rows_ref,
    t_ref,
    basis_buf,
    coords_ref,
    perm_ref,
    sems,
):
    points = pltpu.make_async_copy(points_ref, coords_ref, sems.at[0])
    first = pltpu.make_async_copy(transfer_ref.at[0], t_ref.at[0], sems.at[1])
    order = pltpu.make_async_copy(order_ref, perm_ref, sems.at[2])
    copies = []
    for leaf in range(2):
        block = pl.ds(leaf * LEAF, LEAF)
        copies.append(
            (
                pltpu.make_async_copy(basis_ref.at[leaf], basis_buf.at[leaf], sems.at[3 + leaf]),
                pltpu.make_async_copy(x_ref.at[block], pack_ref.at[block], sems.at[5 + leaf]),
            )
        )
    points.start()
    for pair in copies:
        for copy in pair:
            copy.start()
    first.start()
    order.start()
    points.wait()
    rows_ref[...] = jnp.concatenate(
        [coords_ref[0], coords_ref[1], jnp.zeros((PACK - ROWS - 4, COLS), BF16)], axis=0
    )
    pack_ref[ROWS:, :] = rows_ref[...]
    total = None
    for leaf in range(2):
        for copy in copies[leaf]:
            copy.wait()
        part = jnp.dot(
            basis_buf[leaf], pack_ref[leaf * LEAF : (leaf + 1) * LEAF, :], preferred_element_type=F32
        )
        total = part if total is None else total + part
    s_ref[...] = total.astype(BF16)
    first.wait()
    order.wait()
    t_ref[0, 1] = folded(t_ref[0, 1], perm_ref[0:1, :])


def project(x, basis_t, coords, transfer, perm):
    return pl.pallas_call(
        project_kernel,
        out_shape=(
            jax.ShapeDtypeStruct((RANK, COLS), BF16),
            jax.ShapeDtypeStruct((PACK, COLS), BF16),
            jax.ShapeDtypeStruct((PACK - ROWS, COLS), BF16),
            jax.ShapeDtypeStruct((1, 2, RANK, RANK), BF16),
        ),
        in_specs=[HBM] * 5,
        out_specs=(VMEM,) * 4,
        scratch_shapes=[
            pltpu.VMEM((2, RANK, LEAF), BF16),
            pltpu.VMEM((2, 2, LEAF), BF16),
            pltpu.VMEM((LEVELS, RANK), jnp.int32),
            pltpu.SemaphoreType.DMA((7,)),
        ],
        compiler_params=params(),
        name="project",
    )(*(in_hbm(array) for array in (x, basis_t, coords, transfer, perm)))


def prepare_kernel(transfer_ref, perm_ref, after_ref, t_ref):
    t_ref[0, 0] = transfer_ref[1, 0]
    t_ref[0, 1] = folded(transfer_ref[1, 1], perm_ref[1:2, :])


def prepare(transfer, perm, after):
    return pl.pallas_call(
        prepare_kernel,
        out_shape=jax.ShapeDtypeStruct((1, 2, RANK, RANK), BF16),
        in_specs=[VMEM, VMEM, VMEM],
        out_specs=VMEM,
        compiler_params=params(),
        name="prepare",
    )(transfer, perm, after)


def level_kernel(t_ref, own_ref, other_ref, s_ref):
    total = jnp.dot(t_ref[0, 0], own_ref[...], preferred_element_type=F32)
    total = total + jnp.dot(t_ref[0, 1], other_ref[...], preferred_element_type=F32)
    s_ref[...] = total.astype(BF16)


def gathered_kernel(high_ref, t_ref, own_ref, both_ref, s_ref):
    total = jnp.dot(t_ref[0, 0], own_ref[...], preferred_element_type=F32)
    total = total + jnp.dot(
        t_ref[0, 1], both_ref[1 - high_ref[0]], preferred_element_type=F32
    )
    s_ref[...] = total.astype(BF16)


def level_step(t, index, own, other, high=None, weight=4 * RANK * RANK * COLS):
    flat = pl.BlockSpec((RANK, COLS), lambda i: (0, 0))
    specs = [pl.BlockSpec((1, 2, RANK, RANK), lambda i: (index, 0, 0, 0)), flat]
    if high is None:
        body, specs, args = level_kernel, specs + [flat], (t, own, other)
    else:
        both = pl.BlockSpec((2, RANK, COLS), lambda i: (0, 0, 0))
        body, specs, args = gathered_kernel, [SMEM] + specs + [both], (high, t, own, other)
    return pl.pallas_call(
        body,
        grid=(1,),
        out_shape=jax.ShapeDtypeStruct((RANK, COLS), BF16),
        in_specs=specs,
        out_specs=flat,
        compiler_params=params(),
        cost_estimate=pl.CostEstimate(
            flops=weight, transcendentals=0, bytes_accessed=6 * RANK * COLS
        ),
        name=f"level_{index}",
    )(*args)


def scaled(rows):
    return rows.astype(F32) * (1.0 / FACTOR)


def wanted(index_ref, target, offset):
    return (
        (index_ref[target, 0] == offset)
        | (index_ref[target, 1] == offset)
        | (index_ref[target, 2] == offset)
    )


def tile_of(columns, rows, target, leaf):
    dx = columns[:, 2 * target : 2 * target + 1] - rows[2 * leaf : 2 * leaf + 1, :]
    dy = columns[:, 2 * target + 1 : 2 * target + 2] - rows[2 * leaf + 1 : 2 * leaf + 2, :]
    return lax.rsqrt(dx * dx + dy * dy + SOFT / FACTOR**2).astype(BF16)


def add_tile(index_ref, near_ref, target, offset, source, leaf, columns, rows):
    @pl.when(wanted(index_ref, target, offset))
    def _():
        held = source[leaf * LEAF : (leaf + 1) * LEAF, :]
        for start in range(0, LEAF, PIECE):
            tile = tile_of(columns[start : start + PIECE], rows, target, leaf)
            near_ref[pl.ds(target * LEAF + start, PIECE), :] += jnp.dot(
                tile, held, preferred_element_type=F32
            )


def own_kernel(
    index_ref, own_ref, rows_ref, expand_ref, transfer_ref, perm_ref, _, near_ref, e_ref, t_ref
):
    for level in range(2, LEVELS):
        t_ref[level - 2, 0] = transfer_ref[level, 0]
        t_ref[level - 2, 1] = folded(transfer_ref[level, 1], perm_ref[level : level + 1, :])
    for leaf in range(2):
        e_ref[leaf * LEAF : (leaf + 1) * LEAF, :] = expand_ref[leaf].T
    near_ref[...] = jnp.zeros((ROWS, COLS), F32)
    rows = scaled(rows_ref[:8, :])
    columns = rows.T
    for target in range(2):
        for leaf in range(2):
            add_tile(index_ref, near_ref, target, leaf - target, own_ref, leaf, columns, rows)


def near_own(index, own, rows, expand_t, transfer, perm, after):
    return pl.pallas_call(
        own_kernel,
        out_shape=(
            jax.ShapeDtypeStruct((ROWS, COLS), F32),
            jax.ShapeDtypeStruct((ROWS, RANK), BF16),
            jax.ShapeDtypeStruct((LEVELS - 2, 2, RANK, RANK), BF16),
        ),
        in_specs=[SMEM] + [VMEM] * 6,
        out_specs=(VMEM,) * 3,
        compiler_params=params(),
        name="near_own",
    )(index, own, rows, expand_t, transfer, perm, after)


def side_kernel(
    test, table_ref, rows_ref, source_ref, _, near_ref, buf, tiles, index_ref, sems
):
    low, high = test(lax.axis_index("wide"), lax.axis_index("pair"))
    spans = ((ROWS, PACK - ROWS), (0, LEAF), (LEAF, LEAF))
    copies = []
    for i, (start, size) in enumerate(spans):
        block = pl.ds(start, size)
        copies.append(pltpu.make_async_copy(source_ref.at[block], buf.at[block], sems.at[i]))
    table = pltpu.make_async_copy(table_ref, index_ref, sems.at[3])

    @pl.when(low | high)
    def _():
        table.start()
        for copy in copies:
            copy.start()

    for shift, present in ((-2, low), (2, high)):

        @pl.when(present)
        def _(shift=shift):
            pairs = [
                (leaf, target, shift + leaf - target)
                for leaf in range(2)
                for target in range(2)
                if abs(shift + leaf - target) <= 2
            ]
            table.wait()
            copies[0].wait()
            columns = scaled(rows_ref[:8, :]).T
            rows = scaled(buf[ROWS : ROWS + 8, :])
            for i, (leaf, target, offset) in enumerate(pairs):

                @pl.when(wanted(index_ref, target, offset))
                def _(i=i, leaf=leaf, target=target):
                    for start in range(0, LEAF, PIECE):
                        tiles[i, start : start + PIECE, :] = tile_of(
                            columns[start : start + PIECE], rows, target, leaf
                        )

            for copy in copies[1:]:
                copy.wait()
            for i, (leaf, target, offset) in enumerate(pairs):

                @pl.when(wanted(index_ref, target, offset))
                def _(i=i, leaf=leaf, target=target):
                    near_ref[target * LEAF : (target + 1) * LEAF, :] += jnp.dot(
                        tiles[i],
                        buf[leaf * LEAF : (leaf + 1) * LEAF, :],
                        preferred_element_type=F32,
                    )


def near_side(name, weight, index, rows, test, source, near):
    return pl.pallas_call(
        functools.partial(side_kernel, test),
        out_shape=jax.ShapeDtypeStruct((ROWS, COLS), F32),
        in_specs=[HBM, VMEM, ANY, VMEM],
        out_specs=VMEM,
        scratch_shapes=[
            pltpu.VMEM((PACK, COLS), BF16),
            pltpu.VMEM((3, LEAF, LEAF), BF16),
            pltpu.SMEM((2, 3), jnp.int32),
            pltpu.SemaphoreType.DMA((4,)),
        ],
        input_output_aliases={3: 0},
        compiler_params=params(),
        cost_estimate=pl.CostEstimate(
            flops=weight, transcendentals=0, bytes_accessed=ROWS * COLS * 8
        ),
        name=name,
    )(in_hbm(index), rows, source, near)


def final_kernel(t_ref, own_ref, other_ref, e_ref, near_ref, out_ref, out_buf, sems):
    total = jnp.dot(t_ref[LEVELS - 3, 0], own_ref[...], preferred_element_type=F32)
    total = total + jnp.dot(t_ref[LEVELS - 3, 1], other_ref[...], preferred_element_type=F32)
    s = total.astype(BF16)
    copies = []
    for i in range(ROWS // CHUNK):
        block = pl.ds(i * CHUNK, CHUNK)
        distant = jnp.dot(e_ref[block, :], s, preferred_element_type=F32)
        out_buf[block, :] = (near_ref[block, :] + distant).astype(BF16)
        copies.append(pltpu.make_async_copy(out_buf.at[block], out_ref.at[block], sems.at[i]))
        copies[-1].start()
    for copy in copies:
        copy.wait()


def final_step(t, own, other, e, near):
    return pl.pallas_call(
        final_kernel,
        out_shape=jax.ShapeDtypeStruct((ROWS, COLS), BF16),
        in_specs=[VMEM] * 5,
        out_specs=HBM,
        scratch_shapes=[
            pltpu.VMEM((ROWS, COLS), BF16),
            pltpu.SemaphoreType.DMA((ROWS // CHUNK,)),
        ],
        compiler_params=params(),
        name="final",
    )(t, own, other, e, near)


def from_partner(block, axis, bit):
    count = lax.axis_size(axis)
    return lax.ppermute(block, axis, [(i, i ^ (1 << bit)) for i in range(count)])


def with_partner(block, axis, bit):
    count = lax.axis_size(axis)
    pairs = [[i, i | 1 << bit] for i in range(count) if not i >> bit & 1]
    both = lax.all_gather(block, axis, axis_index_groups=pairs)
    high = (lax.axis_index(axis) >> bit & 1).reshape(1)
    return both, high


def on_device(rhs, coords, near_index, project_basis, expand_basis, transfer, level_perm):
    axes = ("wide", "pair")
    wide, pair = lax.axis_size("wide"), lax.axis_size("pair")
    devices = wide * pair
    turn = 4 * pair

    def odd(i):
        return i % 2 == 1

    def even(i):
        return (i % 2 == 0) & (i % RUN != 0)

    def outer(i):
        return (i % RUN == 0) & (i % turn != 0)

    def far(i):
        return i % turn == 0

    def swapped(block, keep):
        up = [(i - 1, i) for i in range(1, devices) if keep(i)]
        return lax.ppermute(block, axes, up + [(b, a) for a, b in up])

    def met(keep):
        def test(w, q):
            i = w * pair + q
            return keep(i) & (i > 0), keep(i + 1) & (i + 1 < devices)

        return test

    s, pack, rows, t0 = project(
        rhs, jnp.swapaxes(project_basis, 1, 2), coords, transfer[0], level_perm
    )
    odd_side = swapped(pack, odd)
    both, high_bit = with_partner(s, "wide", 0)
    s = level_step(t0, 0, s, both, high_bit)
    partner = from_partner(s, "wide", 1)
    sent, s = lax.optimization_barrier((pack, s))
    outer_side = swapped(sent, outer)
    even_side = swapped(sent, even)
    t1 = prepare(transfer[0], level_perm, s)
    s = level_step(t1, 0, s, partner, weight=COVER_1)
    partner = from_partner(s, "wide", 2)
    sent, s = lax.optimization_barrier((sent, s))
    far_side = swapped(sent, far)
    near, e, t = near_own(
        near_index, sent, rows, jnp.swapaxes(expand_basis, 1, 2), transfer[0], level_perm, s
    )
    partner, near = lax.optimization_barrier((partner, near))
    s = level_step(t, 0, s, partner)
    both, high_bit = with_partner(s, "pair", 0)
    s = level_step(t, 1, s, both, high_bit)
    partner = from_partner(s, "pair", 1)

    for name, weight, keep, side in (
        ("near_odd", COVER_ODD, odd, in_hbm(odd_side)),
        ("near_even", COVER_EVEN, even, in_hbm(even_side)),
        ("near_outer", COVER_OUTER, outer, in_hbm(outer_side)),
        ("near_far", COVER_FAR, far, far_side),
    ):
        near = near_side(name, weight, near_index, rows, met(keep), side, near)
    return final_step(t, s, partner, e, near)


def solution(mesh):
    return jax.shard_map(
        on_device,
        mesh=mesh,
        in_specs=(
            P(("wide", "pair"), None),
            P(("wide", "pair"), None, None),
            P(("wide", "pair"), None),
            P(("wide", "pair"), None, None),
            P(("wide", "pair"), None, None),
            P(("wide", "pair"), None, None, None, None),
            P(),
        ),
        out_specs=P(("wide", "pair"), None),
        check_vma=False,
    )
```
